32 devices in a mesh: wide: 8 (over z, y), section: 4 (over x, core).
Axes of the slice: x: 2, y: 2, z: 4, core: 2. Of those that a mesh axis runs over, the one named last changes fastest.
Arguments:
- tokens: bfloat16 [64, 16384], P('wide', 'section'), may hold values from -6 to 6
- gate_kept: bfloat16 [8192, 32768], P('section', 'wide'), may hold values from -0.0625 to 0.0625
- up_kept: bfloat16 [8192, 32768], P('section', 'wide'), may hold values from -0.0625 to 0.0625
- gate_keep: int32 [128, 32768], P('section', 'wide'), may hold values from 0 to 5
- up_keep: int32 [128, 32768], P('section', 'wide'), may hold values from 0 to 5
- down_weight: bfloat16 [32768, 16384], P('wide', 'section'), may hold values from -0.03125 to 0.03125
Outputs:
- next_input: bfloat16 [64, 16384], P('wide', 'section')
- gram: float32 [16384, 16384], P('section', 'wide')
The draws below stay inside these ranges and needn't reach their ends.
Inputs may be any that keep to these rules, and one draw needn't show every extreme that they name: `gate_keep`: a pattern code names one of the six pairs of positions kept in each group of four input rows. `up_keep`: a pattern code names one of the six pairs of positions kept in each group of four input rows.
All inputs are finite; a program needn't handle non-finite values.
Results may differ from the reference program's by a relative error of at most 0.0063.
Values may be sent and summed in bfloat16 or wider, within the bound.
No kernel may reach another device: no remote copies, remote signals or barrier semaphores. Data moves between devices by JAX's collectives and lax.ppermute only.
A program may use at most 320 MiB of HBM per device.

```python
import jax
import jax.numpy as jnp
from jax import lax

D = 16384
FF = 32768
KEEP_BLOCK = 128
TOKENS = 64


def with_ends(result, rng, least, largest):
    index_at = [jax.random.randint(jax.random.fold_in(rng, axis), (), 0, length) for axis, length in enumerate(result.shape)]
    main_axis = result.shape.index(max(result.shape))
    beside = index_at[:main_axis] + [(index_at[main_axis] + 1) % result.shape[main_axis]] + index_at[main_axis + 1:]
    return result.at[tuple(index_at)].set(least).at[tuple(beside)].set(largest)


def block_scale(own_key, dims, shards, smallest, top_value):
    factor_of, own = 1.0, jax.random.fold_in(own_key, 6)
    for dim, shards_of in shards:
        heights = jnp.exp(jax.random.uniform(jax.random.fold_in(own, dim), (shards_of,), jnp.float32, smallest / len(shards), top_value / len(shards)))
        factor_of = factor_of * jnp.repeat(heights, dims[dim] // shards_of).reshape([-1 if axis == dim else 1 for axis in range(len(dims))])
    return factor_of


def scatter_about(rng, extent, spread, most, shards=(), kind=jnp.bfloat16):
    result = spread * jax.random.normal(rng, extent, jnp.float32)
    if shards:
        result = result * block_scale(rng, extent, shards, -0.22, 0.18)
    return jnp.clip(result, -most, most).astype(kind)


def setup_inputs(seed: int = 0) -> dict:
    key_list = jax.random.split(jax.random.key(seed), 7)
    tokens = scatter_about(key_list[0], (TOKENS, D), 1.0, 6.0, ((0, 8), (1, 4)))
    gate_kept = scatter_about(key_list[1], (D // 2, FF), (D // 2) ** -0.5, 0.0625, ((0, 4), (1, 8)))
    up_kept = scatter_about(key_list[2], (D // 2, FF), (D // 2) ** -0.5, 0.0625, ((0, 4), (1, 8)))
    gate_keep = with_ends(jax.random.randint(key_list[3], (D // KEEP_BLOCK, FF), 0, 6), jax.random.fold_in(key_list[3], 1), 0, 5).astype(jnp.int32)
    up_keep = with_ends(jax.random.randint(key_list[4], (D // KEEP_BLOCK, FF), 0, 6), jax.random.fold_in(key_list[4], 1), 0, 5).astype(jnp.int32)
    down_weight = scatter_about(key_list[5], (FF, D), FF ** -0.5, 0.03125, ((0, 8), (1, 4)))
    return dict(tokens=tokens, gate_kept=gate_kept, up_kept=up_kept, gate_keep=gate_keep, up_keep=up_keep, down_weight=down_weight)


def expand(kept, codes):
    blocks = codes.shape[0]
    width = kept.shape[1]
    pairs = kept.reshape(blocks, 32, 2, width)
    kinds = jnp.arange(6, dtype=jnp.int32)[:, None, None]
    table_first = jnp.array([0, 0, 0, 1, 1, 2], dtype=jnp.int32)[:, None, None]
    table_second = jnp.array([1, 2, 3, 2, 3, 3], dtype=jnp.int32)[:, None, None]
    match = (codes[None, :, :] == kinds).astype(jnp.int32)
    first = lax.optimization_barrier(jnp.sum(table_first * match, axis=0))
    second = lax.optimization_barrier(jnp.sum(table_second * match, axis=0))
    position = lax.broadcasted_iota(jnp.int32, (1, 1, 4, 1), 2)
    zero = jnp.zeros((), kept.dtype)
    dense = jnp.where(position == first[:, None, None, :], pairs[:, :, 0:1, :], zero)
    dense = dense + jnp.where(position == second[:, None, None, :], pairs[:, :, 1:2, :], zero)
    return dense.reshape(blocks * 128, width)

def reference(tokens, gate_kept, up_kept, gate_keep, up_keep, down_weight):
    block_width = min(FF, 2048)
    total = jnp.zeros((tokens.shape[0], D), jnp.float32)
    for number in range(FF // block_width):
        begin = number * block_width
        gate_dense = expand(gate_kept[:, begin:begin + block_width], gate_keep[:, begin:begin + block_width])
        up_dense = expand(up_kept[:, begin:begin + block_width], up_keep[:, begin:begin + block_width])
        gate = jnp.dot(tokens, gate_dense, preferred_element_type=jnp.float32)
        up_val = jnp.dot(tokens, up_dense, preferred_element_type=jnp.float32)
        hidden = (jax.nn.silu(gate) * up_val).astype(jnp.bfloat16)
        total = total + jnp.dot(hidden, down_weight[begin:begin + block_width], preferred_element_type=jnp.float32)
    next_input = total.astype(jnp.bfloat16)
    gram = lax.dot_general(next_input, next_input, (((0,), (0,)), ((), ())), preferred_element_type=jnp.float32)
    gram = gram * (1.0 / jnp.sqrt(jnp.float32(TOKENS)))
    return (next_input, gram)
```

```python
import functools
import math

import jax
import jax.numpy as jnp
from jax import lax
from jax.experimental import pallas as pl
from jax.experimental.pallas import tpu as pltpu
from jax.sharding import PartitionSpec as P

F32, BF16 = jnp.float32, jnp.bfloat16
ROWS, GROUP = 128, 4
MIB = 1 << 20


def tile(limit, width):
    return limit if width % limit == 0 else width


def call(kernel, name, grid, scalars, inputs, outputs, scratch=(), cost=(0, 0), vmem=48):
    arrays, in_specs = zip(*inputs)
    shapes, out_specs = zip(*outputs)
    return pl.pallas_call(
        kernel,
        name=name,
        grid_spec=pltpu.PrefetchScalarGridSpec(
            num_scalar_prefetch=1,
            grid=grid,
            in_specs=list(in_specs),
            out_specs=list(out_specs),
            scratch_shapes=list(scratch),
        ),
        out_shape=list(shapes),
        cost_estimate=pl.CostEstimate(flops=cost[0], bytes_accessed=cost[1], transcendentals=0),
        compiler_params=pltpu.CompilerParams(vmem_limit_bytes=vmem * MIB),
    )(scalars, *arrays)


def whole(shape):
    return pl.BlockSpec(shape, lambda *_: (0,) * len(shape))


def arrange_kernel(near, where, *refs):
    own, other, out = refs[:near], refs[near:2 * near], refs[2 * near]
    deep = 2 * ROWS
    row = lax.broadcasted_iota(jnp.int32, (deep, 3 * ROWS), 0)
    column = lax.broadcasted_iota(jnp.int32, (deep, 3 * ROWS), 1)
    kind, lane = column // ROWS, column % ROWS
    block, group, second = lane // (ROWS // 2), (lane % (ROWS // 2)) // 2, lane % 2
    place = jnp.where(second == 0, kind, 3 - kind)
    mix = jnp.where(row == block * ROWS + group * GROUP + place, 1.0, 0.0).astype(BF16)
    chunks = own[0].shape[1] // deep
    first = where[2] == 0
    for k in range(near):
        a, b = own[k][...].astype(F32), other[k][...].astype(F32)
        both = jnp.concatenate((jnp.where(first, a, b), jnp.where(first, b, a)), axis=0).astype(BF16)
        rows = both.shape[0]
        flat = jnp.concatenate([both[:, deep * i:deep * (i + 1)] for i in range(chunks)], axis=0)
        mixed = jnp.dot(flat, mix, preferred_element_type=F32).astype(BF16)
        at = pl.multiple_of((where[1] ^ k) * rows, rows)
        for i in range(chunks):
            for n in range(3):
                out[n, pl.ds(at, rows), ROWS * i:ROWS * (i + 1)] = mixed[rows * i:rows * (i + 1), ROWS * n:ROWS * (n + 1)]


def share_kernel(where, tokens, gate, up, gate_code, up_code, out, place):
    depth, width = gate.shape
    blocks = gate_code.shape[0]
    kept = depth // blocks
    many = 4 if blocks % 4 == 0 else 1
    even = lax.broadcasted_iota(jnp.int32, (16, width), 0) % 2 == 0
    for side, (values, codes) in enumerate(((gate, gate_code), (up, up_code))):
        code = codes[...]
        place[0] = jnp.where(code < 3, 0.0, jnp.where(code < 5, 1.0, 2.0))
        place[1] = jnp.where(code == 0, 2.0, jnp.where((code == 1) | (code == 3), 1.0, 0.0))
        total = jnp.zeros(out.shape[1:], F32)
        for q in range(blocks // many):
            parts = ([], [], [])
            for k in range(many * q, many * (q + 1)):
                first = jnp.broadcast_to(place[0, pl.ds(k, 1), :], (16, width))
                second = jnp.broadcast_to(place[1, pl.ds(k, 1), :], (16, width))
                kind = jnp.where(even, first, second)
                value = values[kept * k:kept * (k + 1), :]
                for n in range(3):
                    mask = jnp.where(kind == n, 1.0, 0.0).astype(BF16)
                    parts[n].append(value * jnp.concatenate([mask] * (kept // 16), axis=0))
            span = many * kept
            for n in range(3):
                part = jnp.concatenate(parts[n], axis=0)
                total = total + jnp.dot(tokens[n, :, span * q:span * (q + 1)], part, preferred_element_type=F32)
        out[side] = total


def down_kernel(count, adds, where, *refs):
    hidden, weights, rest = refs[:count], refs[count:2 * count], refs[2 * count:]
    total = rest[0][...] if adds else None
    for left, right in zip(hidden, weights):
        product = jnp.dot(left[...], right[...], preferred_element_type=F32)
        total = product if total is None else total + product
    rest[-1][...] = total.astype(rest[-1].dtype)


def split_kernel(where, mine, theirs, *outs):
    rows = outs[0].shape[0]
    for k, out in enumerate(outs):
        at = pl.ds(pl.multiple_of((where[1] ^ k) * rows, rows), rows)
        out[...] = (mine[at, :] + theirs[at, :].astype(F32)).astype(out.dtype)


def finish_kernel(where, *refs):
    total = refs[0][...]
    for ref in refs[1:-1]:
        total = total + ref[...].astype(F32)
    refs[-1][...] = total.astype(BF16)


def join_kernel(where, *refs):
    out = refs[-1]
    rows = refs[0].shape[0]
    for k, ref in enumerate(refs[:-1]):
        out[pl.ds(pl.multiple_of((where[1] ^ k) * rows, rows), rows), :] = ref[...]


def gram_kernel(scale, per, where, own, other, columns, out, tokens_out):
    step = pl.program_id(0)
    rows = out.shape[0]
    half = own.shape[1] // rows
    at = pl.ds(pl.multiple_of((step % half) * rows, rows), rows)
    block = jnp.where(step < half, own[:, at], other[:, at])
    product = lax.dot_general(block, columns[...], (((0,), (0,)), ((), ())), preferred_element_type=F32)
    out[...] = product * scale

    @pl.when(step == 0)
    def _():
        count = tokens_out.shape[0]
        pick = pl.ds(pl.multiple_of(where[1] * 2 * count, 2 * count), 2 * count)
        width = columns.shape[1]
        for index, ref in enumerate((own, other)):
            both = ref[pick, :].astype(F32)
            lines = jnp.where(where[2] == 0, both[:count], both[count:]).astype(BF16)
            for j in range(per):
                side = where[2] ^ index
                to = pl.ds(pl.multiple_of((2 * j + side) * width, width), width)
                tokens_out[:, to] = lines[:, width * j:width * (j + 1)]


def on_device(tokens, gate_kept, up_kept, gate_keep, up_keep, down_weight):
    wide, groups = lax.axis_size("wide"), lax.axis_size("section")
    deep, across = wide // 2, groups // 2
    w, s = lax.axis_index("wide"), lax.axis_index("section")
    z, y, x, c = w // 2, w % 2, s // 2, s % 2
    near = deep <= 4
    kept_rows, local_hidden = gate_kept.shape
    blocks = gate_keep.shape[0]
    own_tokens, section_width = tokens.shape
    count = own_tokens * wide
    share = local_hidden // groups
    half = section_width // 2
    column_width = section_width * groups // wide
    runs = half // column_width

    def scalars(*more):
        return jnp.stack([jnp.asarray(v, jnp.int32) for v in (w, z, y) + more])

    base = scalars()
    pairs = [(i, i ^ 1) for i in range(wide)]
    swap_y = lambda v: lax.ppermute(v, "wide", pairs)
    swap_core = lambda v: lax.ppermute(v, "section", [(i, i ^ 1) for i in range(groups)])
    turn_x = lambda v, j: lax.ppermute(v, "section", [(i, (i + 2 * j) % groups) for i in range(groups)])
    hop_z = lambda v, k: lax.ppermute(v, "wide", [(i, i ^ (2 * k)) for i in range(wide)])
    lines = [[2 * i + e for i in range(deep)] for e in range(2)]

    if near:
        own = [tokens] + [hop_z(tokens, k) for k in range(1, deep)]
        stacked = swap_y(jnp.concatenate(own, axis=0))
        other = [stacked[own_tokens * k:own_tokens * (k + 1)] for k in range(deep)]
        order = base
    else:
        gathered = lax.all_gather(tokens, "wide", axis=0, tiled=True).reshape(deep, 2, own_tokens, section_width)
        own = [gathered[k, 0] for k in range(deep)]
        other = [gathered[k, 1] for k in range(deep)]
        order = jnp.zeros_like(base)
    paired = jax.ShapeDtypeStruct((3, count, section_width // 2), BF16)
    (arranged,) = call(
        functools.partial(arrange_kernel, deep), "arrange", (1,), order,
        [(v, whole(v.shape)) for v in own + other], [(paired, whole(paired.shape))],
    )

    width = tile(512, share)
    steps = share // width

    def partial_share(to_x, to_c):
        q = to_x * 2 + to_c
        piece = lambda rows: pl.BlockSpec((rows, width), lambda j, where: (0, where[3] * steps + j))
        (out,) = call(
            share_kernel, "share", (steps,), scalars(q),
            [(arranged, whole(arranged.shape)), (gate_kept, piece(kept_rows)), (up_kept, piece(kept_rows)),
             (gate_keep, piece(blocks)), (up_keep, piece(blocks))],
            [(jax.ShapeDtypeStruct((2, count, share), F32), pl.BlockSpec((2, count, width), lambda j, where: (0, 0, j)))],
            [pltpu.VMEM((2, blocks, width), F32)],
            cost=(12 * count * kept_rows * share, 4 * kept_rows * share),
        )
        return out

    arrived = []
    for j in range(1, across + 1):
        to_x = (x + j) % across
        sent = swap_core(partial_share(to_x, c ^ 1))
        mine = partial_share(to_x, c)
        if j < across:
            arrived.append(turn_x(mine + sent, j))
    total = mine + sent
    for value in arrived:
        total = total + value
    quarter = (jax.nn.silu(total[0]) * total[1]).astype(BF16)

    block = tile(512, column_width)
    ratio = column_width // block

    def down(hidden, order, adds, side, dtype):
        place = scalars(*order, y if side is None else (y ^ side))
        n = len(hidden)
        if side is None:
            column = lambda j, where: j
        else:
            column = lambda j, where: ((j // ratio) * 2 + where[3 + n]) * ratio + j % ratio
        size = section_width if side is None else half
        inputs = [(v, whole(v.shape)) for v in hidden]
        inputs += [(down_weight, pl.BlockSpec((share, block), functools.partial(lambda i, j, where: (where[3 + i], column(j, where)), i))) for i in range(n)]
        if adds is not None:
            inputs.append((adds, pl.BlockSpec((count, block), lambda j, where: (0, column(j, where)))))
        (out,) = call(
            functools.partial(down_kernel, n, adds is not None), "down", (size // block,), place, inputs,
            [(jax.ShapeDtypeStruct((count, size), dtype), pl.BlockSpec((count, block), lambda j, where: (0, j)))],
            cost=(2 * count * share * size * n, 2 * share * size * n),
        )
        return out

    beside = swap_core(quarter)
    far = [turn_x(quarter, j) for j in range(1, across)]
    near_sum = down([quarter, beside], [x * 2 + c, x * 2 + (c ^ 1)], None, None, F32)
    more, more_order = [], []
    for j in range(1, across):
        from_x = (x - j) % across
        more += [far[j - 1], swap_core(far[j - 1])]
        more_order += [from_x * 2 + c, from_x * 2 + (c ^ 1)]
    sent = swap_y(down(more, more_order, near_sum, 1, BF16))
    mine = down(more, more_order, near_sum, 0, F32)

    rows = count // deep
    if near:
        piece = lambda dtype: (jax.ShapeDtypeStruct((rows, half), dtype), whole((rows, half)))
        parts = call(
            split_kernel, "split", (1,), base, [(mine, whole(mine.shape)), (sent, whole(sent.shape))],
            [piece(F32)] + [piece(BF16)] * (deep - 1),
        )
        parts = [parts[0]] + [hop_z(v, k) for k, v in enumerate(parts) if k]
        (final,) = call(finish_kernel, "finish", (1,), base, [(v, whole(v.shape)) for v in parts], [piece(BF16)])
        pieces = [final] + [hop_z(final, k) for k in range(1, deep)]
        joined = jax.ShapeDtypeStruct((count, half), BF16)
        (ours,) = call(join_kernel, "join", (1,), base, [(v, whole(v.shape)) for v in pieces], [(joined, whole(joined.shape))])
    else:
        both = (mine + sent.astype(F32)).astype(BF16)
        parts = lax.all_to_all(both, "wide", 0, 0, tiled=True, axis_index_groups=lines)
        final = jnp.sum(parts.reshape(deep, rows, half).astype(F32), axis=0).astype(BF16)
        ours = lax.all_gather(final, "wide", axis=0, tiled=True, axis_index_groups=lines)
    theirs = swap_y(ours)

    per = wide // groups
    root = [i // per for i in range(wide)]
    at_root = w // per
    held = lax.dynamic_slice_in_dim(ours, ((w % per) // 2) * column_width, column_width, 1)
    held = jnp.where(s == at_root, held, 0).astype(BF16)
    everywhere = ("wide", "section")
    same_core = held
    for j in range(1, across):
        step = [(i * groups + root[i], i * groups + (root[i] + 2 * j) % groups) for i in range(wide)]
        same_core = same_core + lax.ppermute(held, everywhere, step)
    columns = same_core + jnp.where((s ^ at_root) % 2 == 0, 0, swap_core(same_core)).astype(BF16)

    line = tile(512, column_width)
    each = column_width // line

    def natural(i, where):
        side, j = i // (half // line), i % (half // line)
        return ((j // each) * 2 + (where[2] ^ side)) * each + j % each

    gram, next_input = call(
        functools.partial(gram_kernel, 1.0 / math.sqrt(count), runs), "gram", (section_width // line,), base,
        [(ours, whole(ours.shape)), (theirs, whole(theirs.shape)), (columns, whole(columns.shape))],
        [(jax.ShapeDtypeStruct((section_width, column_width), F32), pl.BlockSpec((line, column_width), lambda i, where: (natural(i, where), 0))),
         (jax.ShapeDtypeStruct((own_tokens, section_width), BF16), whole((own_tokens, section_width)))],
        cost=(2 * count * section_width * column_width, 4 * section_width * column_width),
    )
    return (next_input, gram)


def solution(mesh):
    return jax.shard_map(
        on_device,
        mesh=mesh,
        in_specs=(
            P("wide", "section"),
            P("section", "wide"),
            P("section", "wide"),
            P("section", "wide"),
            P("section", "wide"),
            P("wide", "section"),
        ),
        out_specs=(P("wide", "section"), P("section", "wide")),
        check_vma=False,
    )
```

```python
import functools
import math

import jax
import jax.numpy as jnp
from jax import lax
from jax.experimental import pallas as pl
from jax.experimental.pallas import tpu as pltpu
from jax.sharding import PartitionSpec as P


F32, BF16 = jnp.float32, jnp.bfloat16
ROWS, GROUP = 128, 4
MIB = 1 << 20


def tile(limit, width):
    return limit if width % limit == 0 else width


def call(kernel, grid, scalars, inputs, outputs, scratch=(), cost=(0, 0), vmem=4):
    arrays, in_specs = zip(*inputs)
    shapes, out_specs = zip(*outputs)
    return pl.pallas_call(
        kernel,
        grid_spec=pltpu.PrefetchScalarGridSpec(
            num_scalar_prefetch=1,
            grid=grid,
            in_specs=list(in_specs),
            out_specs=list(out_specs),
            scratch_shapes=list(scratch),
        ),
        out_shape=list(shapes),
        cost_estimate=pl.CostEstimate(flops=cost[0], bytes_accessed=cost[1], transcendentals=0),
        compiler_params=pltpu.CompilerParams(vmem_limit_bytes=vmem * MIB),
    )(scalars, *arrays)


def whole(shape):
    return pl.BlockSpec(shape, lambda *_: (0,) * len(shape))


def arrange_kernel(deep_axis, near, where, *refs):
    own, other, out = refs[:deep_axis], refs[deep_axis:2 * deep_axis], refs[2 * deep_axis]
    deep = 2 * ROWS
    row = lax.broadcasted_iota(jnp.int32, (deep, 3 * ROWS), 0)
    column = lax.broadcasted_iota(jnp.int32, (deep, 3 * ROWS), 1)
    kind, lane = column // ROWS, column % ROWS
    block, group, second = lane // (ROWS // 2), (lane % (ROWS // 2)) // 2, lane % 2
    place = jnp.where(second == 0, kind, 3 - kind)
    mix = jnp.where(row == block * ROWS + group * GROUP + place, 1.0, 0.0).astype(BF16)
    chunks = own[0].shape[1] // deep
    first = (where[2] == 0) if near else True
    for k in range(deep_axis):
        a, b = own[k][...].astype(F32), other[k][...].astype(F32)
        both = jnp.concatenate((jnp.where(first, a, b), jnp.where(first, b, a)), axis=0).astype(BF16)
        rows = both.shape[0]
        flat = jnp.concatenate([both[:, deep * i:deep * (i + 1)] for i in range(chunks)], axis=0)
        mixed = jnp.dot(flat, mix, preferred_element_type=F32).astype(BF16)
        at = pl.multiple_of(((where[1] ^ k) if near else k) * rows, rows)
        for i in range(chunks):
            for n in range(3):
                out[n, pl.ds(at, rows), ROWS * i:ROWS * (i + 1)] = mixed[rows * i:rows * (i + 1), ROWS * n:ROWS * (n + 1)]


def share_kernel(across, ahead, turn, where, tokens, gate, up, gate_code, up_code, out, held, held_code, place, here, code_here):
    depth, share = held.shape[1:]
    blocks = held_code.shape[1]
    kept = depth // blocks
    many = 4 if blocks % 4 == 0 else 1
    span = many * kept
    lanes = tile(512, share)
    start = pl.multiple_of((lax.rem(where[3] + ahead, across) * 2 + (where[4] ^ turn)) * share, share)
    piece, ahead_by = tile(512, depth), 4
    code_copies = [
        pltpu.make_async_copy(source.at[:, pl.ds(start, share)], held_code.at[side], code_here.at[side])
        for side, source in enumerate((gate_code, up_code))
    ]
    copies, index = [], {}
    for side, source in enumerate((gate, up)):
        for at in range(0, share, lanes):
            for row in range(0, depth, piece):
                index[side, at, row] = len(copies)
                copies.append(pltpu.make_async_copy(
                    source.at[pl.ds(row, piece), pl.ds(start + at, lanes)],
                    held.at[side, pl.ds(row, piece), pl.ds(at, lanes)], here.at[len(copies)],
                ))
    code_copies[0].start()
    for copy in copies[:ahead_by]:
        copy.start()
    code_copies[1].start()
    even = lax.broadcasted_iota(jnp.int32, (16, lanes), 0) % 2 == 0
    for side in range(2):
        code_copies[side].wait()
        code = held_code[side]
        place[side, 0] = jnp.where(code < 3, 0.0, jnp.where(code < 5, 1.0, 2.0))
        place[side, 1] = jnp.where(code == 0, 2.0, jnp.where((code == 1) | (code == 3), 1.0, 0.0))
        for at in range(0, share, lanes):
            part_lanes = slice(at, at + lanes)
            total = jnp.zeros((out.shape[1], lanes), F32)
            for row in range(0, depth, span):
                number = index.get((side, at, row))
                if number is not None:
                    copies[number].wait()
                    if number + ahead_by < len(copies):
                        copies[number + ahead_by].start()
                parts = ([], [], [])
                for k in range(row // kept, (row + span) // kept):
                    first = jnp.broadcast_to(place[side, 0, pl.ds(k, 1), part_lanes], (16, lanes))
                    second = jnp.broadcast_to(place[side, 1, pl.ds(k, 1), part_lanes], (16, lanes))
                    kind = jnp.where(even, first, second)
                    value = held[side, kept * k:kept * (k + 1), part_lanes]
                    for n in range(3):
                        mask = jnp.where(kind == n, 1.0, 0.0).astype(BF16)
                        parts[n].append(value * jnp.concatenate([mask] * (kept // 16), axis=0))
                for n in range(3):
                    part = jnp.concatenate(parts[n], axis=0)
                    total = total + jnp.dot(tokens[n, :, row:row + span], part, preferred_element_type=F32)
            out[side, :, part_lanes] = total


def fetch_kernel(across, ahead, where, source, out, arrived):
    pieces = arrived.shape[0]
    rows = out.shape[0] // pieces
    start = lax.rem(where[3] + (across - ahead), across) * out.shape[0]
    copies = [
        pltpu.make_async_copy(
            source.at[pl.ds(pl.multiple_of(start + rows * i, rows), rows), :], out.at[pl.ds(rows * i, rows), :], arrived.at[i]
        )
        for i in range(pieces)
    ]
    for copy in copies:
        copy.start()
    for copy in copies:
        copy.wait()


def down_kernel(runs, side, where, own, beside, weights, *rest):
    adds, out = rest[:-1], rest[-1]
    share = own.shape[1]
    full = weights.shape[1]
    run = full // (2 * runs)
    lanes = tile(512, run)
    for i in range(out.shape[1] // lanes):
        at = i * lanes
        if side is not None:
            column = pl.ds(pl.multiple_of((2 * (at // run) + (where[2] ^ side)) * run + at % run, lanes), lanes)
        else:
            column = pl.ds(at, lanes)
        total = adds[0][:, column] if adds else None
        for left, core in ((own, where[4]), (beside, where[4] ^ 1)):
            right = weights[pl.ds(pl.multiple_of(core * share, share), share), column]
            product = jnp.dot(left[...], right, preferred_element_type=F32)
            total = product if total is None else total + product
        out[:, pl.ds(at, lanes)] = total.astype(out.dtype)


def split_kernel(where, mine, theirs, *outs):
    rows = outs[0].shape[0]
    for k, out in enumerate(outs):
        at = pl.ds(pl.multiple_of((where[1] ^ k) * rows, rows), rows)
        out[...] = (mine[at, :] + theirs[at, :].astype(F32)).astype(out.dtype)


def finish_kernel(where, *refs):
    total = refs[0][...]
    for ref in refs[1:-1]:
        total = total + ref[...].astype(F32)
    refs[-1][...] = total.astype(BF16)


def join_kernel(where, *refs):
    out = refs[-1]
    rows = refs[0].shape[0]
    for k, ref in enumerate(refs[:-1]):
        out[pl.ds(pl.multiple_of((where[1] ^ k) * rows, rows), rows), :] = ref[...]


def gram_kernel(scale, per, where, own, other, columns, out, tokens_out):
    step = pl.program_id(0)
    rows = out.shape[0]
    half = own.shape[1] // rows
    at = pl.ds(pl.multiple_of((step % half) * rows, rows), rows)
    block = jnp.where(step < half, own[:, at], other[:, at])
    product = lax.dot_general(block, columns[...], (((0,), (0,)), ((), ())), preferred_element_type=F32)
    out[...] = product * scale

    @pl.when(step == 0)
    def _():
        count = tokens_out.shape[0]
        pick = pl.ds(pl.multiple_of(where[1] * 2 * count, 2 * count), 2 * count)
        width = columns.shape[1]
        for index, ref in enumerate((own, other)):
            both = ref[pick, :].astype(F32)
            lines = jnp.where(where[2] == 0, both[:count], both[count:]).astype(BF16)
            for j in range(per):
                side = where[2] ^ index
                to = pl.ds(pl.multiple_of((2 * j + side) * width, width), width)
                tokens_out[:, to] = lines[:, width * j:width * (j + 1)]


def on_device(tokens, gate_kept, up_kept, gate_keep, up_keep, down_weight):
    wide, groups = lax.axis_size("wide"), lax.axis_size("section")
    deep, across = wide // 2, groups // 2
    w, s = lax.axis_index("wide"), lax.axis_index("section")
    z, y, x, c = w // 2, w % 2, s // 2, s % 2
    near = deep <= 4
    kept_rows, local_hidden = gate_kept.shape
    blocks = gate_keep.shape[0]
    own_tokens, section_width = tokens.shape
    count = own_tokens * wide
    half = section_width // 2
    column_width = section_width * groups // wide
    runs = half // column_width

    base = jnp.stack([jnp.asarray(v, jnp.int32) for v in (w, z, y, x, c)])
    gate_kept, up_kept, gate_keep, up_keep, down_weight = (
        pltpu.with_memory_space_constraint(v, pltpu.HBM) for v in (gate_kept, up_kept, gate_keep, up_keep, down_weight)
    )
    pairs = [(i, i ^ 1) for i in range(wide)]

    swap_y = lambda v: lax.ppermute(v, "wide", pairs)
    swap_core = lambda v: lax.ppermute(v, "section", [(i, i ^ 1) for i in range(groups)])
    turn_x = lambda v, j: lax.ppermute(v, "section", [(i, (i + 2 * j) % groups) for i in range(groups)])
    hop_z = lambda v, k: lax.ppermute(v, "wide", [(i, i ^ (2 * k)) for i in range(wide)])
    lines = [[2 * i + e for i in range(deep)] for e in range(2)]

    if near:
        own = [tokens] + [hop_z(tokens, k) for k in range(1, deep)]
        stacked = swap_y(jnp.concatenate(own, axis=0))
        other = [stacked[own_tokens * k:own_tokens * (k + 1)] for k in range(deep)]
    else:
        gathered = lax.all_gather(tokens, "wide", axis=0, tiled=True).reshape(deep, 2, own_tokens, section_width)
        own = [gathered[k, 0] for k in range(deep)]
        other = [gathered[k, 1] for k in range(deep)]
    paired = jax.ShapeDtypeStruct((3, count, section_width // 2), BF16)
    (arranged,) = call(
        functools.partial(arrange_kernel, deep, near), (1,), base,
        [(v, whole(v.shape)) for v in own + other], [(paired, whole(paired.shape))],
    )

    share = local_hidden // groups
    held_rows = []
    for j in range(across):
        (rows_held,) = call(
            functools.partial(fetch_kernel, across, j), (), base, [(down_weight, pl.BlockSpec(memory_space=pltpu.HBM))],
            [(pltpu.VMEM((2 * share, section_width), BF16), pl.BlockSpec(memory_space=pltpu.VMEM))],
            [pltpu.SemaphoreType.DMA((8,))], cost=(0, 4 * share * section_width), vmem=2,
        )
        held_rows.append(pltpu.with_memory_space_constraint(rows_held, pltpu.VMEM))

    in_hbm, in_vmem = pl.BlockSpec(memory_space=pltpu.HBM), pl.BlockSpec(memory_space=pltpu.VMEM)

    def partial_share(ahead, turn):
        (out,) = call(
            functools.partial(share_kernel, across, ahead, turn), (), base,
            [(arranged, in_vmem)] + [(v, in_hbm) for v in (gate_kept, up_kept, gate_keep, up_keep)],
            [(jax.ShapeDtypeStruct((2, count, share), F32), in_vmem)],
            [pltpu.VMEM((2, kept_rows, share), BF16), pltpu.VMEM((2, blocks, share), jnp.int32),
             pltpu.VMEM((2, 2, blocks, share), F32), pltpu.SemaphoreType.DMA((2 * (share // tile(512, share)) * (kept_rows // tile(512, kept_rows)),)),
             pltpu.SemaphoreType.DMA((2,))],
            cost=(12 * count * kept_rows * share, 4 * kept_rows * share), vmem=12,
        )
        return out

    arrived = []
    for j in range(1, across + 1):
        sent = swap_core(partial_share(j, 1))
        mine = partial_share(j, 0)
        if j < across:
            arrived.append(turn_x(mine + sent, j))
    total = mine + sent
    for value in arrived:
        total = total + value
    quarter = (jax.nn.silu(total[0]) * total[1]).astype(BF16)

    def down(own, beside, weights, adds, side, dtype):
        size = section_width if side is None else half
        inputs = [(v, whole(v.shape)) for v in (own, beside)] + [(weights, pl.BlockSpec(memory_space=pltpu.VMEM))]
        if adds is not None:
            inputs.append((adds, whole(adds.shape)))
        (out,) = call(
            functools.partial(down_kernel, runs, side), (), base, inputs,
            [(jax.ShapeDtypeStruct((count, size), dtype), whole((count, size)))],
            cost=(4 * count * share * size, 4 * share * size), vmem=4,
        )
        return out

    beside = swap_core(quarter)
    far = [turn_x(quarter, j) for j in range(1, across)]
    total = down(quarter, beside, held_rows[0], None, None, F32)
    for j in range(1, across):
        value = far[j - 1]
        other_core = swap_core(value)
        if j < across - 1:
            total = down(value, other_core, held_rows[j], total, None, F32)
    sent = swap_y(down(value, other_core, held_rows[-1], total, 1, BF16))
    mine = down(value, other_core, held_rows[-1], total, 0, F32)

    rows = count // deep
    if near:
        piece = lambda dtype: (jax.ShapeDtypeStruct((rows, half), dtype), whole((rows, half)))
        parts = call(
            split_kernel, (1,), base, [(mine, whole(mine.shape)), (sent, whole(sent.shape))],
            [piece(F32)] + [piece(BF16)] * (deep - 1),
        )
        parts = [parts[0]] + [hop_z(v, k) for k, v in enumerate(parts) if k]
        (final,) = call(finish_kernel, (1,), base, [(v, whole(v.shape)) for v in parts], [piece(BF16)])
        pieces = [final] + [hop_z(final, k) for k in range(1, deep)]
        joined = jax.ShapeDtypeStruct((count, half), BF16)
        (ours,) = call(join_kernel, (1,), base, [(v, whole(v.shape)) for v in pieces], [(joined, whole(joined.shape))])
    else:
        both = (mine + sent.astype(F32)).astype(BF16)
        parts = lax.all_to_all(both, "wide", 0, 0, tiled=True, axis_index_groups=lines)
        final = jnp.sum(parts.reshape(deep, rows, half).astype(F32), axis=0).astype(BF16)
        ours = lax.all_gather(final, "wide", axis=0, tiled=True, axis_index_groups=lines)
    theirs = swap_y(ours)

    per = wide // groups
    root = [i // per for i in range(wide)]
    at_root = w // per
    held = lax.dynamic_slice_in_dim(ours, ((w % per) // 2) * column_width, column_width, 1)
    held = jnp.where(s == at_root, held, 0).astype(BF16)
    everywhere = ("wide", "section")
    same_core = held
    for j in range(1, across):
        step = [(i * groups + root[i], i * groups + (root[i] + 2 * j) % groups) for i in range(wide)]
        same_core = same_core + lax.ppermute(held, everywhere, step)
    columns = same_core + jnp.where((s ^ at_root) % 2 == 0, 0, swap_core(same_core)).astype(BF16)

    line = tile(512, column_width)
    each = column_width // line

    def natural(i, where):
        side, j = i // (half // line), i % (half // line)
        return ((j // each) * 2 + (where[2] ^ side)) * each + j % each

    gram, next_input = call(
        functools.partial(gram_kernel, 1.0 / math.sqrt(count), runs), (section_width // line,), base,
        [(ours, whole(ours.shape)), (theirs, whole(theirs.shape)), (columns, whole(columns.shape))],
        [(jax.ShapeDtypeStruct((section_width, column_width), F32), pl.BlockSpec((line, column_width), lambda i, where: (natural(i, where), 0))),
         (jax.ShapeDtypeStruct((own_tokens, section_width), BF16), whole((own_tokens, section_width)))],
        cost=(2 * count * section_width * column_width, 4 * section_width * column_width), vmem=40,
    )
    return (next_input, gram)


def solution(mesh):
    return jax.shard_map(
        on_device,
        mesh=mesh,
        in_specs=(
            P("wide", "section"),
            P("section", "wide"),
            P("section", "wide"),
            P("section", "wide"),
            P("section", "wide"),
            P("wide", "section"),
        ),
        out_specs=(P("wide", "section"), P("section", "wide")),
        check_vma=False,
    )
```

```python
import functools
import math

import jax
import jax.numpy as jnp
from jax import lax
from jax.experimental import pallas as pl
from jax.experimental.pallas import tpu as pltpu
from jax.sharding import PartitionSpec as P


F32, BF16 = jnp.float32, jnp.bfloat16
ROWS, GROUP = 128, 4
MIB = 1 << 20


def tile(limit, width):
    return limit if width % limit == 0 else width


def call(kernel, grid, scalars, inputs, outputs, scratch=(), cost=(0, 0), vmem=4):
    arrays, in_specs = zip(*inputs)
    shapes, out_specs = zip(*outputs)
    return pl.pallas_call(
        kernel,
        grid_spec=pltpu.PrefetchScalarGridSpec(
            num_scalar_prefetch=1,
            grid=grid,
            in_specs=list(in_specs),
            out_specs=list(out_specs),
            scratch_shapes=list(scratch),
        ),
        out_shape=list(shapes),
        cost_estimate=pl.CostEstimate(flops=cost[0], bytes_accessed=cost[1], transcendentals=0),
        compiler_params=pltpu.CompilerParams(vmem_limit_bytes=vmem * MIB),
    )(scalars, *arrays)


def whole(shape):
    return pl.BlockSpec(shape, lambda *_: (0,) * len(shape))


def arrange_kernel(deep_axis, near, where, *refs):
    own, other, out = refs[:deep_axis], refs[deep_axis:2 * deep_axis], refs[2 * deep_axis]
    deep = 2 * ROWS
    row = lax.broadcasted_iota(jnp.int32, (deep, 3 * ROWS), 0)
    column = lax.broadcasted_iota(jnp.int32, (deep, 3 * ROWS), 1)
    kind, lane = column // ROWS, column % ROWS
    block, group, second = lane // (ROWS // 2), (lane % (ROWS // 2)) // 2, lane % 2
    place = jnp.where(second == 0, kind, 3 - kind)
    mix = jnp.where(row == block * ROWS + group * GROUP + place, 1.0, 0.0).astype(BF16)
    chunks = own[0].shape[1] // deep
    first = (where[2] == 0) if near else True
    for k in range(deep_axis):
        a, b = own[k][...].astype(F32), other[k][...].astype(F32)
        both = jnp.concatenate((jnp.where(first, a, b), jnp.where(first, b, a)), axis=0).astype(BF16)
        rows = both.shape[0]
        flat = jnp.concatenate([both[:, deep * i:deep * (i + 1)] for i in range(chunks)], axis=0)
        mixed = jnp.dot(flat, mix, preferred_element_type=F32).astype(BF16)
        at = pl.multiple_of(((where[1] ^ k) if near else k) * rows, rows)
        for i in range(chunks):
            for n in range(3):
                out[n, pl.ds(at, rows), ROWS * i:ROWS * (i + 1)] = mixed[rows * i:rows * (i + 1), ROWS * n:ROWS * (n + 1)]


def fetches(across, first, where, source, out, share, arrived):
    pieces = arrived.shape[0]
    rows = out.shape[0] // pieces
    copies = []
    for i in range(pieces):
        quarter, row = first + rows * i // share, rows * i % share
        start = (lax.rem(where[3] + (across - quarter // 2), across) * 2 + quarter % 2) * share + row
        copies.append(pltpu.make_async_copy(
            source.at[pl.ds(pl.multiple_of(start, rows), rows), :], out.at[pl.ds(rows * i, rows), :], arrived.at[i]
        ))
    return copies


def fetch_kernel(across, first, share, where, source, out, arrived):
    copies = fetches(across, first, where, source, out, share, arrived)
    for copy in copies:
        copy.start()
    for copy in copies:
        copy.wait()


def share_kernel(across, ahead, turn, where, tokens, gate, up, gate_code, up_code, out, held, place, here):
    tiles, depth, lanes = held.shape
    blocks = gate_code.shape[0]
    kept = depth // blocks
    many = 4 if blocks % 4 == 0 else 1
    span = many * kept
    per = tiles // 2
    pieces = here.shape[1]
    piece = depth // pieces
    start = (lax.rem(where[3] + ahead, across) * 2 + (where[4] ^ turn)) * per * lanes

    def columns(t):
        return pl.ds(pl.multiple_of(start + lax.rem(t, per) * lanes, lanes), lanes)

    def kept_copy(source, t, p):
        rows = pl.ds(p * piece, piece)
        return pltpu.make_async_copy(source.at[rows, columns(t)], held.at[t, rows, :], here.at[t, p])

    def begin(values, t):
        for p in range(pieces):
            kept_copy(values, t, p).start()

    even = lax.broadcasted_iota(jnp.int32, (16, lanes), 0) % 2 == 0
    begin(gate, 0)

    def one(t, carry):
        @pl.when(t + 1 < per)
        def _():
            begin(gate, t + 1)

        @pl.when((t + 1 >= per) & (t + 1 < tiles))
        def _():
            begin(up, t + 1)

        code = jnp.where(t < per, gate_code[:, columns(t)], up_code[:, columns(t)])
        place[0] = jnp.where(code < 3, 0.0, jnp.where(code < 5, 1.0, 2.0))
        place[1] = jnp.where(code == 0, 2.0, jnp.where((code == 1) | (code == 3), 1.0, 0.0))
        total = jnp.zeros((out.shape[1], lanes), F32)
        for row in range(0, depth, span):
            if row % piece == 0:
                kept_copy(gate, t, row // piece).wait()
            parts = ([], [], [])
            for k in range(row // kept, (row + span) // kept):
                first = jnp.broadcast_to(place[0, pl.ds(k, 1), :], (16, lanes))
                second = jnp.broadcast_to(place[1, pl.ds(k, 1), :], (16, lanes))
                kind = jnp.where(even, first, second)
                value = held[t, kept * k:kept * (k + 1), :]
                for n in range(3):
                    mask = jnp.where(kind == n, 1.0, 0.0).astype(BF16)
                    parts[n].append(value * jnp.concatenate([mask] * (kept // 16), axis=0))
            for n in range(3):
                part = jnp.concatenate(parts[n], axis=0)
                total = total + jnp.dot(tokens[n, :, row:row + span], part, preferred_element_type=F32)
        out[lax.div(t, per), :, pl.ds(pl.multiple_of(lax.rem(t, per) * lanes, lanes), lanes)] = total
        return carry

    lax.fori_loop(0, tiles, one, 0)


def down_kernel(runs, side, flips, base, where, *refs):
    uses = len(flips)
    hidden, weights, adds, out = refs[:uses], refs[uses], refs[uses + 1:-1], refs[-1]
    share = hidden[0].shape[1]
    run = weights.shape[1] // (2 * runs)
    lanes = tile(512, run)
    for i in range(out.shape[1] // lanes):
        at = i * lanes
        if side is not None:
            column = pl.ds(pl.multiple_of((2 * (at // run) + (where[2] ^ side)) * run + at % run, lanes), lanes)
        else:
            column = pl.ds(at, lanes)
        total = None
        for ref in adds:
            total = ref[:, pl.ds(at, lanes) if ref.shape[1] == out.shape[1] else column]
        for left, flip in zip(hidden, flips):
            rows = pl.ds(pl.multiple_of(base + (where[4] ^ flip) * share, share), share)
            product = jnp.dot(left[...], weights[rows, column], preferred_element_type=F32)
            total = product if total is None else total + product
        out[:, pl.ds(at, lanes)] = total.astype(out.dtype)


def split_kernel(where, mine, theirs, *outs):
    rows = outs[0].shape[0]
    for k, out in enumerate(outs):
        at = pl.ds(pl.multiple_of((where[1] ^ k) * rows, rows), rows)
        out[...] = (mine[at, :] + theirs[at, :].astype(F32)).astype(out.dtype)


def finish_kernel(where, *refs):
    total = refs[0][...]
    for ref in refs[1:-1]:
        total = total + ref[...].astype(F32)
    refs[-1][...] = total.astype(BF16)


def join_kernel(where, *refs):
    out = refs[-1]
    rows = refs[0].shape[0]
    for k, ref in enumerate(refs[:-1]):
        out[pl.ds(pl.multiple_of((where[1] ^ k) * rows, rows), rows), :] = ref[...]


def gram_kernel(scale, runs, where, own, other, columns, out, tokens_out, held, gone):
    parts, rows = held.shape[1:3]
    width = columns.shape[1]
    line = parts * rows
    steps = own.shape[1] // line
    each = width // line

    def copy(step, side, j, part):
        at = (((j // each) * 2 + (where[2] ^ side)) * each + j % each) * line + part * rows
        slot = lax.rem(step, 2)
        return pltpu.make_async_copy(held.at[slot, part], out.at[pl.ds(pl.multiple_of(at, rows), rows), :], gone.at[slot, part])

    for side, ref in enumerate((own, other)):
        def one(j, carry):
            step = side * steps + j
            slot = lax.rem(step, 2)
            for part in range(parts):
                pl.when(step >= 2)(copy(step, side, j, part).wait)
                at = pl.ds(pl.multiple_of(j * line + part * rows, rows), rows)
                product = lax.dot_general(ref[:, at], columns[...], (((0,), (0,)), ((), ())), preferred_element_type=F32)
                held[slot, part] = product * scale
                copy(step, side, j, part).start()
            return carry

        lax.fori_loop(0, steps, one, 0)
    count = tokens_out.shape[0]
    pick = pl.ds(pl.multiple_of(where[1] * 2 * count, 2 * count), 2 * count)
    for index, ref in enumerate((own, other)):
        both = ref[pick, :].astype(F32)
        lines = jnp.where(where[2] == 0, both[:count], both[count:]).astype(BF16)
        for j in range(runs):
            to = pl.ds(pl.multiple_of((2 * j + (where[2] ^ index)) * width, width), width)
            tokens_out[:, to] = lines[:, width * j:width * (j + 1)]
    for step in range(2 * steps - 2, 2 * steps):
        for part in range(parts):
            copy(step, 1, step - steps, part).wait()


def on_device(tokens, gate_kept, up_kept, gate_keep, up_keep, down_weight):
    wide, groups = lax.axis_size("wide"), lax.axis_size("section")
    deep, across = wide // 2, groups // 2
    w, s = lax.axis_index("wide"), lax.axis_index("section")
    z, y, x, c = w // 2, w % 2, s // 2, s % 2
    near = deep <= 4
    kept_rows, local_hidden = gate_kept.shape
    blocks = gate_keep.shape[0]
    own_tokens, section_width = tokens.shape
    count = own_tokens * wide
    half = section_width // 2
    column_width = section_width * groups // wide
    runs = half // column_width

    base = jnp.stack([jnp.asarray(v, jnp.int32) for v in (w, z, y, x, c)])
    gate_kept, up_kept, gate_keep, up_keep, down_weight = (
        pltpu.with_memory_space_constraint(v, space)
        for v, space in (
            (gate_kept, pltpu.HBM), (up_kept, pltpu.HBM), (gate_keep, pltpu.VMEM), (up_keep, pltpu.VMEM), (down_weight, pltpu.HBM),
        )
    )
    pairs = [(i, i ^ 1) for i in range(wide)]

    swap_y = lambda v: lax.ppermute(v, "wide", pairs)
    swap_core = lambda v: lax.ppermute(v, "section", [(i, i ^ 1) for i in range(groups)])
    turn_x = lambda v, j: lax.ppermute(v, "section", [(i, (i + 2 * j) % groups) for i in range(groups)])
    hop_z = lambda v, k: lax.ppermute(v, "wide", [(i, i ^ (2 * k)) for i in range(wide)])
    lines = [[2 * i + e for i in range(deep)] for e in range(2)]

    if near:
        own = [tokens] + [hop_z(tokens, k) for k in range(1, deep)]
        stacked = swap_y(jnp.concatenate(own, axis=0))
        other = [stacked[own_tokens * k:own_tokens * (k + 1)] for k in range(deep)]
    else:
        gathered = lax.all_gather(tokens, "wide", axis=0, tiled=True).reshape(deep, 2, own_tokens, section_width)
        own = [gathered[k, 0] for k in range(deep)]
        other = [gathered[k, 1] for k in range(deep)]
    paired = jax.ShapeDtypeStruct((3, count, section_width // 2), BF16)
    (arranged,) = call(
        functools.partial(arrange_kernel, deep, near), (1,), base,
        [(v, whole(v.shape)) for v in own + other], [(paired, whole(paired.shape))],
    )

    share = local_hidden // groups
    in_hbm, in_vmem = pl.BlockSpec(memory_space=pltpu.HBM), pl.BlockSpec(memory_space=pltpu.VMEM)
    held_rows = []
    for start, many in ((0, 2), (2, groups - 2)):
        (rows_held,) = call(
            functools.partial(fetch_kernel, across, start, share), (), base, [(down_weight, in_hbm)],
            [(pltpu.VMEM((many * share, section_width), BF16), in_vmem)],
            [pltpu.SemaphoreType.DMA((2 * many,))], cost=(0, 2 * many * share * section_width), vmem=2,
        )
        held_rows.append(pltpu.with_memory_space_constraint(rows_held, pltpu.VMEM))

    lanes = tile(512, share)
    tiles, pieces = 2 * share // lanes, kept_rows // tile(1024, kept_rows)

    def partial_share(ahead, turn):
        (out,) = call(
            functools.partial(share_kernel, across, ahead, turn), (), base,
            [(arranged, in_vmem), (gate_kept, in_hbm), (up_kept, in_hbm), (gate_keep, in_vmem), (up_keep, in_vmem)],
            [(jax.ShapeDtypeStruct((2, count, share), F32), in_vmem)],
            [pltpu.VMEM((tiles, kept_rows, lanes), BF16), pltpu.VMEM((2, blocks, lanes), F32), pltpu.SemaphoreType.DMA((tiles, pieces))],
            cost=(12 * count * kept_rows * share, 4 * kept_rows * share), vmem=12,
        )
        return out

    arrived = []
    for j in range(1, across + 1):
        sent = swap_core(partial_share(j, 1))
        mine = partial_share(j, 0)
        if j < across:
            arrived.append(turn_x(mine + sent, j))
    total = mine + sent
    for value in arrived:
        total = total + value
    quarter = (jax.nn.silu(total[0]) * total[1]).astype(BF16)

    def down(group, hidden, flips, adds, side, dtype):
        size = section_width if side is None else half
        weights = held_rows[0] if group == 0 else held_rows[1]
        start = 0 if group == 0 else 2 * share * (group - 1)
        inputs = [(v, in_vmem) for v in hidden + [weights]] + [(v, in_vmem) for v in adds]
        (out,) = call(
            functools.partial(down_kernel, runs, side, flips, start), (), base, inputs,
            [(jax.ShapeDtypeStruct((count, size), dtype), in_vmem)],
            cost=(2 * len(hidden) * count * share * size, 2 * len(hidden) * share * size), vmem=4,
        )
        return out

    beside = swap_core(quarter)
    far = [turn_x(quarter, j) for j in range(1, across)]
    total = down(0, [quarter, beside], (0, 1), [], None, F32)
    for j in range(1, across):
        value = far[j - 1]
        other_core = swap_core(value)
        if j < across - 1:
            total = down(j, [value, other_core], (0, 1), [total], None, F32)
    last = across - 1
    begun = down(last, [value], (0,), [total], 1, F32)
    sent = swap_y(down(last, [other_core], (1,), [begun], 1, BF16))
    mine = down(last, [value, other_core], (0, 1), [total], 0, F32)

    rows = count // deep
    if near:
        piece = lambda dtype: (jax.ShapeDtypeStruct((rows, half), dtype), whole((rows, half)))
        parts = call(
            split_kernel, (1,), base, [(mine, whole(mine.shape)), (sent, whole(sent.shape))],
            [piece(F32)] + [piece(BF16)] * (deep - 1),
        )
        parts = [parts[0]] + [hop_z(v, k) for k, v in enumerate(parts) if k]
        (final,) = call(finish_kernel, (1,), base, [(v, whole(v.shape)) for v in parts], [piece(BF16)])
        pieces = [final] + [hop_z(final, k) for k in range(1, deep)]
        joined = jax.ShapeDtypeStruct((count, half), BF16)
        (ours,) = call(join_kernel, (1,), base, [(v, whole(v.shape)) for v in pieces], [(joined, whole(joined.shape))])
    else:
        both = (mine + sent.astype(F32)).astype(BF16)
        parts = lax.all_to_all(both, "wide", 0, 0, tiled=True, axis_index_groups=lines)
        final = jnp.sum(parts.reshape(deep, rows, half).astype(F32), axis=0).astype(BF16)
        ours = lax.all_gather(final, "wide", axis=0, tiled=True, axis_index_groups=lines)
    theirs = swap_y(ours)

    per = wide // groups
    root = [i // per for i in range(wide)]
    at_root = w // per
    held = lax.dynamic_slice_in_dim(ours, ((w % per) // 2) * column_width, column_width, 1)
    held = jnp.where(s == at_root, held, 0).astype(BF16)
    everywhere = ("wide", "section")
    same_core = held
    for j in range(1, across):
        step = [(i * groups + root[i], i * groups + (root[i] + 2 * j) % groups) for i in range(wide)]
        same_core = same_core + lax.ppermute(held, everywhere, step)
    columns = same_core + jnp.where((s ^ at_root) % 2 == 0, 0, swap_core(same_core)).astype(BF16)

    line = tile(512, column_width)
    parts = 2
    gram, next_input = call(
        functools.partial(gram_kernel, 1.0 / math.sqrt(count), runs), (), base,
        [(v, in_vmem) for v in (ours, theirs, columns)],
        [(jax.ShapeDtypeStruct((section_width, column_width), F32), in_hbm),
         (jax.ShapeDtypeStruct((own_tokens, section_width), BF16), in_vmem)],
        [pltpu.VMEM((2, parts, line // parts, column_width), F32), pltpu.SemaphoreType.DMA((2, parts))],
        cost=(2 * count * section_width * column_width, 4 * section_width * column_width), vmem=24,
    )
    return (next_input, gram)


def solution(mesh):
    return jax.shard_map(
        on_device,
        mesh=mesh,
        in_specs=(
            P("wide", "section"),
            P("section", "wide"),
            P("section", "wide"),
            P("section", "wide"),
            P("section", "wide"),
            P("wide", "section"),
        ),
        out_specs=(P("wide", "section"), P("section", "wide")),
        check_vma=False,
    )
```
